128 devices in a mesh: row: 16 (over y_lo, x, core), col: 8 (over y_hi, z).
Axes of the slice: x: 4, y: 4 (y_hi: 2, y_lo: 2; y = y_hi * 2 + y_lo), z: 4, core: 2. Of those that a mesh axis runs over, the one named last changes fastest.
Arguments:
- features: bfloat16 [32768, 256], P(('row', 'col')), may hold values from -6 to 6
- adjacency: bfloat16 [128, 384, 128, 128], P(('row', 'col')), may hold values from -0.046875 to 0.046875
- tile_row: int32 [128, 384], P(('row', 'col')), may hold values from 0 to 15, as said below
- tile_column: int32 [128, 384], P(('row', 'col')), may hold values from 0 to 31, as said below
- tile_count: int32 [128], P(('row', 'col')), may hold values from 1 to 384, as said below
- weight_in: bfloat16 [256, 1024], replicated, may hold values from -0.375 to 0.375
- bias_in: float32 [1024], replicated, may hold values from -3 to 3
- weight_out: bfloat16 [1024, 256], replicated, may hold values from -0.25 to 0.25
- bias_out: float32 [256], replicated, may hold values from -3 to 3
Outputs:
- updated: bfloat16 [32768, 256], P(('row', 'col'))
The draws below stay inside these ranges and needn't reach their ends.
Inputs may be any that keep to these rules, and one draw needn't show every extreme that they name: `tile_row`: for every device and slot s < tile_count, the block row i and block column j of step one satisfy i >= j, and no device names one pair twice. Slots at or beyond tile_count hold coordinates in range that are not part of A. Every device of the highest index along row holds exactly 384 tiles. `tile_column`: see tile_row. `tile_count`: every device of the highest index along row has the most.
All inputs are finite; a program needn't handle non-finite values.
Results may differ from the reference program's by a relative error of at most 0.0056.
Values may be sent and summed in bfloat16 or wider, within the bound.
No kernel may reach another device: no remote copies, remote signals or barrier semaphores. Data moves between devices by JAX's collectives and lax.ppermute only.
A program may use at most 128 MiB of HBM per device.

```python
import jax
import jax.numpy as jnp
from jax import lax

TILE = 128
F = 256
HID = 1024
BLK_DEV = 2
BLOCKS = 256
VERTICES = 32768
ROW_BLOCKS = 16
COL_BLOCKS = 32
CAP = 384
DEVICES = 128


def tile_layout(key):
    base = jax.random.fold_in(key, 11)
    col_count = ROW_BLOCKS // BLK_DEV
    device_count = BLOCKS // BLK_DEV
    row_count = device_count // col_count
    pairs = ROW_BLOCKS * COL_BLOCKS

    def one_device(device):
        row_index = device // col_count
        col_index = device % col_count
        candidate = jnp.arange(pairs, dtype=jnp.int32)
        local_rows = candidate // COL_BLOCKS
        local_cols = candidate % COL_BLOCKS
        block_i = row_index * ROW_BLOCKS + local_rows
        block_j = (local_cols // BLK_DEV * col_count + col_index) * BLK_DEV + local_cols % BLK_DEV
        valid = block_i >= block_j
        priority = jax.random.permutation(jax.random.fold_in(base, device), pairs).astype(jnp.int32)
        score = jnp.where(valid, priority, priority + pairs)
        picked = jnp.argsort(score)[:CAP]
        filled = jnp.minimum(jnp.sum(valid.astype(jnp.int32)), CAP).astype(jnp.int32)
        keep = jnp.arange(CAP, dtype=jnp.int32) < filled
        rows_out = jnp.where(keep, local_rows[picked], 0).astype(jnp.int32)
        cols_out = jnp.where(keep, local_cols[picked], 0).astype(jnp.int32)
        lowest = jnp.maximum(filled // 2, 1).astype(jnp.int32)
        drawn = jax.random.randint(jax.random.fold_in(base, device + 100003), (), lowest, filled + 1).astype(jnp.int32)
        count = jnp.where(row_index == row_count - 1, filled, drawn).astype(jnp.int32)
        return (rows_out, cols_out, count)
    return jax.vmap(one_device)(jnp.arange(device_count, dtype=jnp.int32))


def draw_tile_row(key, part):
    return tile_layout(key)[0]


def draw_tile_column(key, part):
    return tile_layout(key)[1]


def draw_tile_count(key, part):
    return tile_layout(key)[2]


def levels(rng, shape, split, low, top_value):
    def one(position, shards_of):
        heights = jax.random.uniform(jax.random.fold_in(jax.random.fold_in(rng, 6), position), (shards_of,), jnp.float32, low / len(split), top_value / len(split))
        return jnp.repeat(jnp.exp(heights), shape[position] // shards_of).reshape((-1,) + (1,) * (len(shape) - position - 1))

    level = one(*split[0])
    for cut in split[1:]:
        level = level * one(*cut)
    return level


def noise(own_key, extent, scale, reach, pieces=(), held_as=jnp.bfloat16):
    values = scale * jax.random.normal(own_key, extent, jnp.float32)
    if pieces:
        values = values * levels(own_key, extent, pieces, -0.22, 0.18)
    return jnp.clip(values, -reach, reach).astype(held_as)


def setup_inputs(seed: int = 0) -> dict:
    splits = jax.random.split(jax.random.key(seed), 10)
    features = noise(splits[0], (VERTICES, F), 1.0, 6.0, ((0, 128),))
    adjacency = noise(splits[1], (DEVICES, CAP, TILE, TILE), (TILE * BLOCKS // 2) ** -0.5, 0.046875, ((0, 128),))
    tile_row = draw_tile_row(jax.random.fold_in(splits[9], 71), 0)
    tile_column = draw_tile_column(jax.random.fold_in(splits[9], 71), 0)
    tile_count = draw_tile_count(jax.random.fold_in(splits[9], 71), 0)
    weight_in = noise(splits[5], (F, HID), F ** -0.5, 0.375)
    bias_in = noise(splits[6], (HID,), 0.5, 3.0, (), jnp.float32)
    weight_out = noise(splits[7], (HID, F), (HID // 2) ** -0.5, 0.25)
    bias_out = noise(splits[8], (F,), 0.5, 3.0, (), jnp.float32)
    return {"features": features, "adjacency": adjacency, "tile_row": tile_row, "tile_column": tile_column, "tile_count": tile_count, "weight_in": weight_in, "bias_in": bias_in, "weight_out": weight_out, "bias_out": bias_out}


def reference(features, adjacency, tile_row, tile_column, tile_count, weight_in, bias_in, weight_out, bias_out):
    col_count = ROW_BLOCKS // BLK_DEV
    device_count = BLOCKS // BLK_DEV
    vertex_blocks = features.reshape(BLOCKS, TILE, F).astype(jnp.float32)
    slot_index = jnp.arange(CAP, dtype=jnp.int32)

    def per_device(total, device):
        row_index = device // col_count
        col_index = device % col_count
        local_rows = tile_row[device].astype(jnp.int32)
        local_cols = tile_column[device].astype(jnp.int32)
        block_i = (row_index * ROW_BLOCKS + local_rows).astype(jnp.int32)
        block_j = (((local_cols // BLK_DEV) * col_count + col_index) * BLK_DEV + local_cols % BLK_DEV).astype(jnp.int32)
        live = (slot_index < tile_count[device]).astype(jnp.float32)
        tile_values = adjacency[device].astype(jnp.float32)
        to_rows = jnp.einsum("kab,kbf->kaf", tile_values, vertex_blocks[block_j], precision=lax.Precision.HIGHEST)
        to_cols = jnp.einsum("kab,kaf->kbf", tile_values, vertex_blocks[block_i], precision=lax.Precision.HIGHEST)
        to_rows = to_rows * live[:, None, None]
        to_cols = to_cols * live[:, None, None]
        total = total.at[block_i].add(to_rows).at[block_j].add(to_cols)
        return total, None

    start = jnp.zeros((BLOCKS, TILE, F), jnp.float32)
    total, _ = lax.scan(per_device, start, jnp.arange(device_count, dtype=jnp.int32))
    combined = (features.astype(jnp.float32) + total.reshape(VERTICES, F)).astype(jnp.bfloat16)
    hidden = jax.nn.relu(jnp.dot(combined, weight_in, preferred_element_type=jnp.float32) + bias_in).astype(jnp.bfloat16)
    updated = jnp.dot(hidden, weight_out, preferred_element_type=jnp.float32) + bias_out
    return updated.astype(jnp.bfloat16)
```

```python
import functools

import jax
import jax.numpy as jnp
from jax import lax
from jax.experimental import pallas as pl
from jax.experimental.pallas import tpu as pltpu
from jax.sharding import PartitionSpec as P


T = 128
BLK = 256
ROWS = 16
COLS = 32
CAP = 384
CHUNKS = 12
CT = CAP // CHUNKS
UNROLL = 16
HOPS = (0, 1, 3, 2)
BF = jnp.bfloat16
F32 = jnp.float32
MIB = 2**20
VMEM = pl.BlockSpec(memory_space=pltpu.VMEM)
SMEM = pl.BlockSpec(memory_space=pltpu.SMEM)
ANY = pl.BlockSpec(memory_space=pl.ANY)
SDS = jax.ShapeDtypeStruct


def row_perm(value, move):
    pairs = []
    for y in range(2):
        for x in range(4):
            for e in range(2):
                ty, tx, te = move(y, x, e)
                pairs.append(((y * 4 + x) * 2 + e, (ty * 4 + tx) * 2 + te))
    return lax.ppermute(value, "row", pairs)


def col_perm(value, move):
    pairs = []
    for y in range(2):
        for z in range(4):
            ty, tz = move(y, z)
            pairs.append((y * 4 + z, ty * 4 + tz))
    return lax.ppermute(value, "col", pairs)


def to_x(value, d):
    return row_perm(value, lambda y, x, e: (y, (x + d) % 4, e))


def to_ylo(value):
    return row_perm(value, lambda y, x, e: (1 - y, x, e))


def to_core(value):
    return row_perm(value, lambda y, x, e: (y, x, 1 - e))


def to_z(value, d):
    return col_perm(value, lambda y, z: (y, (z + d) % 4))


def to_yhi(value):
    return col_perm(value, lambda y, z: (1 - y, z))


def dense_kernel(row_s, col_s, count_s, tiles, panel, panel_t, held, sems):
    count = count_s[0]

    def fetch(q):
        part = pl.ds(q * CT, CT)
        return pltpu.make_async_copy(tiles.at[part], held.at[part], sems.at[q])

    for q in range(CHUNKS):
        fetch(q).start()

    def clear(j, _):
        panel[j] = jnp.zeros((ROWS * T, T), BF)
        return 0

    def clear_t(i, _):
        panel_t[i] = jnp.zeros((COLS * T, T), BF)
        return 0

    lax.fori_loop(0, COLS, clear, 0)
    lax.fori_loop(0, ROWS, clear_t, 0)

    def place(s):
        i = row_s[0, s]
        j = col_s[0, s]
        tile = held[s]
        panel[j, pl.ds(pl.multiple_of(i * T, T), T), :] = tile
        panel_t[i, pl.ds(pl.multiple_of(j * T, T), T), :] = tile.T

    for q in range(CHUNKS):
        fetch(q).wait()
        low = q * CT
        live = jnp.clip(count - low, 0, CT)

        def many(g, _, low=low):
            for u in range(UNROLL):
                place(low + g * UNROLL + u)
            return 0

        def one(s, _):
            place(s)
            return 0

        groups = lax.div(live, UNROLL)
        lax.fori_loop(0, groups, many, 0)
        lax.fori_loop(low + groups * UNROLL, low + live, one, 0)


def dense(tiles, rows, cols, count):
    return pl.pallas_call(
        dense_kernel,
        out_shape=(
            pltpu.VMEM((COLS, ROWS * T, T), BF),
            pltpu.VMEM((ROWS, COLS * T, T), BF),
        ),
        in_specs=[SMEM, SMEM, SMEM, ANY],
        out_specs=(VMEM, VMEM),
        scratch_shapes=[pltpu.VMEM((CAP, T, T), BF), pltpu.SemaphoreType.DMA((CHUNKS,))],
        compiler_params=pltpu.CompilerParams(vmem_limit_bytes=16 * MIB),
        cost_estimate=pl.CostEstimate(flops=0, bytes_accessed=45 * MIB, transcendentals=0),
        name="dense",
    )(rows, cols, count, tiles)


def row_place():
    r = lax.axis_index("row")
    return lax.div(r, 8), lax.rem(lax.div(r, 2), 4), lax.rem(r, 2)


def col_place():
    c = lax.axis_index("col")
    return lax.div(c, 4), lax.rem(c, 4)


def row_of(place, hop, flip, swap):
    y, x, e = place
    y = 1 - y if flip else y
    e = 1 - e if swap else e
    return (y * 4 + lax.rem(x + hop, 4)) * 2 + e


def col_of(place, hop, flip):
    y, z = place
    y = 1 - y if flip else y
    return y * 4 + lax.rem(z + hop, 4)


def block_rows(k):
    return pl.ds(pl.multiple_of(k * BLK, BLK), BLK)


def back_kernel(panel_t, *refs, targets):
    sources = refs[:8]
    outs = refs[8:]
    here, there = col_place(), row_place()
    rhs = jnp.concatenate([ref[...] for ref in sources], axis=0)
    order = []
    for hop in HOPS:
        for flip in range(2):
            c = col_of(here, (4 - hop) % 4, flip)
            order += [2 * c, 2 * c + 1]
    for n, (hop, swap) in enumerate(targets):
        lhs = []
        for flip in range(2):
            part = block_rows(row_of(there, hop, flip, swap))
            lhs.append(jnp.concatenate([panel_t[i, part, :] for i in order], axis=1))
        lhs = jnp.concatenate(lhs, axis=0)
        product = jnp.dot(lhs, rhs, preferred_element_type=F32)
        if len(outs) == 1:
            outs[0][n * 2 * BLK : (n + 1) * 2 * BLK, :] = product.astype(BF)
        else:
            outs[n][...] = product.astype(BF)


def back(panel_t, sources, targets, joined):
    n = len(targets)
    if joined:
        out_shape, out_specs = (SDS((n * 2 * BLK, BLK), BF),), (VMEM,)
    else:
        out_shape, out_specs = (SDS((2 * BLK, BLK), BF),) * n, (VMEM,) * n
    return pl.pallas_call(
        functools.partial(back_kernel, targets=targets),
        out_shape=out_shape,
        in_specs=[VMEM] * 9,
        out_specs=out_specs,
        compiler_params=pltpu.CompilerParams(vmem_limit_bytes=20 * MIB),
        cost_estimate=pl.CostEstimate(
            flops=2 * n * 512 * 2048 * 256, bytes_accessed=n * MIB, transcendentals=0
        ),
        name="back",
    )(panel_t, *sources)


def forward_kernel(panel, same, other, *outs, hops):
    here, there = col_place(), row_place()
    rhs = jnp.concatenate([same[...], other[...]], axis=0)
    order = []
    for swap in range(2):
        for hop in HOPS:
            for flip in range(2):
                k = row_of(there, (4 - hop) % 4, flip, swap)
                order += [2 * k, 2 * k + 1]
    for n, hop in enumerate(hops):
        lhs = []
        for flip in range(2):
            part = block_rows(col_of(here, hop, flip))
            lhs.append(jnp.concatenate([panel[j, part, :] for j in order], axis=1))
        lhs = jnp.concatenate(lhs, axis=0)
        product = jnp.dot(lhs, rhs, preferred_element_type=F32)
        outs[n][...] = product.astype(BF)


def forward(panel, same, other, hops):
    n = len(hops)
    return pl.pallas_call(
        functools.partial(forward_kernel, hops=hops),
        out_shape=(SDS((2 * BLK, BLK), BF),) * n,
        in_specs=[VMEM] * 3,
        out_specs=(VMEM,) * n,
        compiler_params=pltpu.CompilerParams(vmem_limit_bytes=20 * MIB),
        cost_estimate=pl.CostEstimate(
            flops=2 * n * 512 * 4096 * 256, bytes_accessed=n * MIB, transcendentals=0
        ),
        name="forward",
    )(panel, same, other)


def join_kernel(recv, *refs):
    own, outs = refs[:4], refs[4:]
    for n in range(4):
        part = recv[n * 2 * BLK : (n + 1) * 2 * BLK, :].astype(F32)
        outs[n][...] = (own[n][...].astype(F32) + part).astype(BF)


def join(recv, own):
    return pl.pallas_call(
        join_kernel,
        out_shape=(SDS((2 * BLK, BLK), BF),) * 4,
        in_specs=[VMEM] * 5,
        out_specs=(VMEM,) * 4,
        name="join",
    )(recv, *own)


def fold_kernel(own, a, b, c, keep, send):
    total = own[...].astype(F32) + a[...].astype(F32) + b[...].astype(F32) + c[...].astype(F32)
    keep[...] = total[:BLK]
    send[...] = total[BLK:].astype(BF)


def fold(own, arrived):
    return pl.pallas_call(
        fold_kernel,
        out_shape=(SDS((BLK, BLK), F32), SDS((BLK, BLK), BF)),
        in_specs=[VMEM] * 4,
        out_specs=(VMEM, VMEM),
        name="fold",
    )(own, *arrived)


def update_kernel(x, keep_a, recv_a, keep_b, recv_b, w_in, b_in, w_out, b_out, out):
    total = x[...].astype(F32) + (keep_a[...] + recv_a[...].astype(F32))
    total = total + (keep_b[...] + recv_b[...].astype(F32))
    combined = total.astype(BF)
    hidden = jnp.dot(combined, w_in[...], preferred_element_type=F32) + b_in[...]
    hidden = jnp.maximum(hidden, 0.0).astype(BF)
    updated = jnp.dot(hidden, w_out[...], preferred_element_type=F32) + b_out[...]
    out[...] = updated.astype(BF)


def update(x, row_part, col_part, w_in, b_in, w_out, b_out):
    return pl.pallas_call(
        update_kernel,
        out_shape=SDS((BLK, BLK), BF),
        in_specs=[VMEM] * 9,
        out_specs=VMEM,
        name="update",
    )(x, *row_part, *col_part, w_in, b_in.reshape(1, -1), w_out, b_out.reshape(1, -1))


def shards(
    features, adjacency, tile_row, tile_column, tile_count, weight_in, bias_in, weight_out, bias_out
):
    flipped = to_yhi(features)
    row_blocks = [features, flipped]
    for d in HOPS[1:]:
        row_blocks += [to_z(features, d), to_z(flipped, d)]
    flipped = to_ylo(features)
    col_blocks = [features, flipped]
    for d in HOPS[1:]:
        col_blocks += [to_x(features, d), to_x(flipped, d)]
    same = jnp.concatenate(col_blocks, axis=0)
    other = to_core(same)

    panel, panel_t = dense(adjacency[0], tile_row, tile_column, tile_count)

    (to_other,) = back(panel_t, row_blocks, tuple((h, 1) for h in HOPS), True)
    from_other = to_core(to_other)
    own = back(panel_t, row_blocks, tuple((h, 0) for h in HOPS), False)
    chip = join(from_other, own)
    arrived = [to_x(chip[n], HOPS[n]) for n in (1, 2, 3)]

    away = forward(panel, same, other, HOPS[1:])
    row_arrived = [to_z(away[n], HOPS[n + 1]) for n in range(3)]
    (stay,) = forward(panel, same, other, HOPS[:1])

    col_keep, col_send = fold(chip[0], arrived)
    col_recv = to_ylo(col_send)
    row_keep, row_send = fold(stay, row_arrived)
    row_recv = to_yhi(row_send)
    return update(
        features,
        (row_keep, row_recv),
        (col_keep, col_recv),
        weight_in,
        bias_in,
        weight_out,
        bias_out,
    )


def solution(mesh):
    placed = (
        P(("row", "col"), None),
        P(("row", "col"), None, None, None),
        P(("row", "col"), None),
        P(("row", "col"), None),
        P(("row", "col")),
        P(),
        P(),
        P(),
        P(),
    )
    return jax.shard_map(
        shards, mesh=mesh, in_specs=placed, out_specs=P(("row", "col"), None), check_vma=False
    )
```

```python
import functools

import jax
import jax.numpy as jnp
from jax import lax
from jax.experimental import pallas as pl
from jax.experimental.pallas import tpu as pltpu
from jax.sharding import PartitionSpec as P


T = 128
BLK = 256
ROWS = 16
COLS = 32
CAP = 384
CHUNKS = 12
CT = CAP // CHUNKS
UNROLL = 16
HOPS = (0, 1, 3, 2)
BF = jnp.bfloat16
F32 = jnp.float32
MIB = 2**20
VMEM = pl.BlockSpec(memory_space=pltpu.VMEM)
HBM = pl.BlockSpec(memory_space=pltpu.HBM)
SDS = jax.ShapeDtypeStruct


def row_perm(value, move):
    pairs = []
    for y in range(2):
        for x in range(4):
            for e in range(2):
                ty, tx, te = move(y, x, e)
                pairs.append(((y * 4 + x) * 2 + e, (ty * 4 + tx) * 2 + te))
    return lax.ppermute(value, "row", pairs)


def col_perm(value, move):
    pairs = []
    for y in range(2):
        for z in range(4):
            ty, tz = move(y, z)
            pairs.append((y * 4 + z, ty * 4 + tz))
    return lax.ppermute(value, "col", pairs)


def to_x(value, d):
    return row_perm(value, lambda y, x, e: (y, (x + d) % 4, e))


def to_ylo(value):
    return row_perm(value, lambda y, x, e: (1 - y, x, e))


def to_core(value):
    return row_perm(value, lambda y, x, e: (y, x, 1 - e))


def to_z(value, d):
    return col_perm(value, lambda y, z: (y, (z + d) % 4))


def to_yhi(value):
    return col_perm(value, lambda y, z: (1 - y, z))


def dense_kernel(places, tiles, panel_out, panel_t, held, panel, place_s, sems, place_sem, out_sem):
    place_copy = pltpu.make_async_copy(places, place_s, place_sem)
    place_copy.start()

    def fetch(q):
        part = pl.ds(q * CT, CT)
        return pltpu.make_async_copy(tiles.at[part], held.at[part], sems.at[q])

    for q in range(CHUNKS):
        fetch(q).start()

    def clear(j, _):
        panel[j] = jnp.zeros((ROWS * T, T), BF)
        return 0

    def clear_t(i, _):
        panel_t[i] = jnp.zeros((COLS * T, T), BF)
        return 0

    lax.fori_loop(0, COLS, clear, 0)
    place_copy.wait()
    count = place_s[0, CAP]

    def spot(s):
        at = place_s[0, s]
        return lax.div(at, COLS), lax.rem(at, COLS)

    def put(s):
        i, j = spot(s)
        panel[j, pl.ds(pl.multiple_of(i * T, T), T), :] = held[s]

    def put_t(s):
        i, j = spot(s)
        panel_t[i, pl.ds(pl.multiple_of(j * T, T), T), :] = held[s].T

    def each(low, live, step):
        def many(g, _):
            for u in range(UNROLL):
                step(low + g * UNROLL + u)
            return 0

        def one(s, _):
            step(s)
            return 0

        groups = lax.div(live, UNROLL)
        lax.fori_loop(0, groups, many, 0)
        lax.fori_loop(low + groups * UNROLL, low + live, one, 0)

    for q in range(CHUNKS):
        fetch(q).wait()
        each(q * CT, jnp.clip(count - q * CT, 0, CT), put)
    out_copy = pltpu.make_async_copy(panel, panel_out, out_sem)
    out_copy.start()
    lax.fori_loop(0, ROWS, clear_t, 0)
    each(0, count, put_t)
    out_copy.wait()


def slots(tile_row, tile_column, tile_count):
    spots = jnp.pad(tile_row * COLS + tile_column, ((0, 0), (0, T)))
    at = lax.broadcasted_iota(jnp.int32, spots.shape, 1)
    return jnp.where(at == CAP, tile_count[0], spots)


def dense(tiles, places):
    return pl.pallas_call(
        dense_kernel,
        out_shape=(
            SDS((COLS, ROWS * T, T), BF),
            pltpu.VMEM((ROWS, COLS * T, T), BF),
        ),
        in_specs=[HBM, HBM],
        out_specs=(HBM, VMEM),
        scratch_shapes=[
            pltpu.VMEM((CAP, T, T), BF),
            pltpu.VMEM((COLS, ROWS * T, T), BF),
            pltpu.SMEM((1, CAP + T), jnp.int32),
            pltpu.SemaphoreType.DMA((CHUNKS,)),
            pltpu.SemaphoreType.DMA,
            pltpu.SemaphoreType.DMA,
        ],
        compiler_params=pltpu.CompilerParams(vmem_limit_bytes=30 * MIB),
        cost_estimate=pl.CostEstimate(flops=0, bytes_accessed=45 * MIB, transcendentals=0),
        name="dense",
    )(places, tiles)


def row_place():
    r = lax.axis_index("row")
    return lax.div(r, 8), lax.rem(lax.div(r, 2), 4), lax.rem(r, 2)


def col_place():
    c = lax.axis_index("col")
    return lax.div(c, 4), lax.rem(c, 4)


def row_of(place, hop, flip, swap):
    y, x, e = place
    y = 1 - y if flip else y
    e = 1 - e if swap else e
    return (y * 4 + lax.rem(x + hop, 4)) * 2 + e


def col_of(place, hop, flip):
    y, z = place
    y = 1 - y if flip else y
    return y * 4 + lax.rem(z + hop, 4)


def block_rows(k):
    return pl.ds(pl.multiple_of(k * BLK, BLK), BLK)


def back_kernel(panel_t, *refs, targets):
    sources = refs[:8]
    outs = refs[8:]
    here, there = col_place(), row_place()
    rhs = jnp.concatenate([ref[...] for ref in sources], axis=0)
    order = []
    for hop in HOPS:
        for flip in range(2):
            c = col_of(here, (4 - hop) % 4, flip)
            order += [2 * c, 2 * c + 1]
    for n, (hop, swap) in enumerate(targets):
        lhs = []
        for flip in range(2):
            k = row_of(there, hop, flip, swap)
            part = block_rows(k)
            lhs.append(jnp.concatenate([panel_t[i, part, :] for i in order], axis=1))
        lhs = jnp.concatenate(lhs, axis=0)
        product = jnp.dot(lhs, rhs, preferred_element_type=F32)
        if len(outs) == 1:
            outs[0][n * 2 * BLK : (n + 1) * 2 * BLK, :] = product.astype(BF)
        else:
            outs[n][...] = product.astype(BF)


def back(panel_t, sources, targets, joined):
    n = len(targets)
    if joined:
        out_shape, out_specs = (SDS((n * 2 * BLK, BLK), BF),), (VMEM,)
    else:
        out_shape, out_specs = (SDS((2 * BLK, BLK), BF),) * n, (VMEM,) * n
    return pl.pallas_call(
        functools.partial(back_kernel, targets=targets),
        out_shape=out_shape,
        in_specs=[VMEM] * 9,
        out_specs=out_specs,
        compiler_params=pltpu.CompilerParams(vmem_limit_bytes=12 * MIB),
        cost_estimate=pl.CostEstimate(
            flops=2 * n * 512 * 2048 * 256, bytes_accessed=n * MIB, transcendentals=0
        ),
        name="back",
    )(panel_t, *sources)


def forward_kernel(panel, same, other, *outs, hops):
    here, there = col_place(), row_place()
    rhs = jnp.concatenate([same[...], other[...]], axis=0)
    order = []
    for swap in range(2):
        for hop in HOPS:
            for flip in range(2):
                k = row_of(there, (4 - hop) % 4, flip, swap)
                order += [2 * k, 2 * k + 1]
    for n, hop in enumerate(hops):
        lhs = []
        for flip in range(2):
            part = block_rows(col_of(here, hop, flip))
            lhs.append(jnp.concatenate([panel[j, part, :] for j in order], axis=1))
        lhs = jnp.concatenate(lhs, axis=0)
        product = jnp.dot(lhs, rhs, preferred_element_type=F32)
        outs[n][...] = product.astype(BF)


def forward(panel, same, other, hops):
    n = len(hops)
    return pl.pallas_call(
        functools.partial(forward_kernel, hops=hops),
        out_shape=(SDS((2 * BLK, BLK), BF),) * n,
        in_specs=[VMEM] * 3,
        out_specs=(VMEM,) * n,
        compiler_params=pltpu.CompilerParams(vmem_limit_bytes=12 * MIB),
        cost_estimate=pl.CostEstimate(
            flops=2 * n * 512 * 4096 * 256, bytes_accessed=n * MIB, transcendentals=0
        ),
        name="forward",
    )(panel, same, other)


def join_kernel(recv, *refs):
    own, outs = refs[:4], refs[4:]
    for n in range(4):
        part = recv[n * 2 * BLK : (n + 1) * 2 * BLK, :].astype(F32)
        outs[n][...] = (own[n][...].astype(F32) + part).astype(BF)


def join(recv, own):
    return pl.pallas_call(
        join_kernel,
        out_shape=(SDS((2 * BLK, BLK), BF),) * 4,
        in_specs=[VMEM] * 5,
        out_specs=(VMEM,) * 4,
        compiler_params=pltpu.CompilerParams(vmem_limit_bytes=4 * MIB),
        name="join",
    )(recv, *own)


def fold_kernel(own, a, b, c, keep, send):
    total = own[...].astype(F32) + a[...].astype(F32) + b[...].astype(F32) + c[...].astype(F32)
    keep[...] = total[:BLK]
    send[...] = total[BLK:].astype(BF)


def fold(own, arrived):
    return pl.pallas_call(
        fold_kernel,
        out_shape=(SDS((BLK, BLK), F32), SDS((BLK, BLK), BF)),
        in_specs=[VMEM] * 4,
        out_specs=(VMEM, VMEM),
        compiler_params=pltpu.CompilerParams(vmem_limit_bytes=4 * MIB),
        name="fold",
    )(own, *arrived)


def update_kernel(x, keep_a, recv_a, keep_b, recv_b, w_in, b_in, w_out, b_out, out):
    total = x[...].astype(F32) + (keep_a[...] + recv_a[...].astype(F32))
    total = total + (keep_b[...] + recv_b[...].astype(F32))
    combined = total.astype(BF)
    hidden = jnp.dot(combined, w_in[...], preferred_element_type=F32) + b_in[...]
    hidden = jnp.maximum(hidden, 0.0).astype(BF)
    updated = jnp.dot(hidden, w_out[...], preferred_element_type=F32) + b_out[...]
    out[...] = updated.astype(BF)


def update(x, row_part, col_part, w_in, b_in, w_out, b_out):
    return pl.pallas_call(
        update_kernel,
        out_shape=SDS((BLK, BLK), BF),
        in_specs=[VMEM] * 9,
        out_specs=VMEM,
        compiler_params=pltpu.CompilerParams(vmem_limit_bytes=4 * MIB),
        name="update",
    )(x, *row_part, *col_part, w_in, b_in.reshape(1, -1), w_out, b_out.reshape(1, -1))


def shards(
    features, adjacency, tile_row, tile_column, tile_count, weight_in, bias_in, weight_out, bias_out
):
    flipped = to_yhi(features)
    row_blocks = [features, flipped]
    for d in HOPS[1:]:
        row_blocks += [to_z(features, d), to_z(flipped, d)]
    flipped = to_ylo(features)
    col_blocks = [features, flipped]
    for d in HOPS[1:]:
        col_blocks += [to_x(features, d), to_x(flipped, d)]
    same = jnp.concatenate(col_blocks, axis=0)
    other = to_core(same)

    places = slots(tile_row, tile_column, tile_count)
    places, row_blocks = lax.optimization_barrier((places, row_blocks))
    panel, panel_t = dense(adjacency[0], places)

    (to_other,) = back(panel_t, row_blocks, tuple((h, 1) for h in HOPS), True)
    from_other = to_core(to_other)
    own = back(panel_t, row_blocks, tuple((h, 0) for h in HOPS), False)
    chip = join(from_other, own)
    arrived = [to_x(chip[n], HOPS[n]) for n in (1, 2, 3)]

    away = forward(panel, same, other, HOPS[1:])
    row_arrived = [to_z(away[n], HOPS[n + 1]) for n in range(3)]
    (stay,) = forward(panel, same, other, HOPS[:1])

    col_keep, col_send = fold(chip[0], arrived)
    col_recv = to_ylo(col_send)
    row_keep, row_send = fold(stay, row_arrived)
    row_recv = to_yhi(row_send)
    return update(
        features,
        (row_keep, row_recv),
        (col_keep, col_recv),
        weight_in,
        bias_in,
        weight_out,
        bias_out,
    )


def solution(mesh):
    placed = (
        P(("row", "col"), None),
        P(("row", "col"), None, None, None),
        P(("row", "col"), None),
        P(("row", "col"), None),
        P(("row", "col")),
        P(),
        P(),
        P(),
        P(),
    )
    return jax.shard_map(
        shards, mesh=mesh, in_specs=placed, out_specs=P(("row", "col"), None), check_vma=False
    )
```

```python
import functools

import jax
import jax.numpy as jnp
from jax import lax
from jax.experimental import pallas as pl
from jax.experimental.pallas import tpu as pltpu
from jax.sharding import PartitionSpec as P


T = 128
BLK = 256
ROWS = 16
COLS = 32
CAP = 384
CHUNKS = 12
CT = CAP // CHUNKS
UNROLL = 16
HOPS = (0, 1, 3, 2)
BF = jnp.bfloat16
F32 = jnp.float32
MIB = 2**20
VMEM = pl.BlockSpec(memory_space=pltpu.VMEM)
HBM = pl.BlockSpec(memory_space=pltpu.HBM)
SDS = jax.ShapeDtypeStruct


def row_perm(value, move):
    pairs = []
    for y in range(2):
        for x in range(4):
            for e in range(2):
                ty, tx, te = move(y, x, e)
                pairs.append(((y * 4 + x) * 2 + e, (ty * 4 + tx) * 2 + te))
    return lax.ppermute(value, "row", pairs)


def col_perm(value, move):
    pairs = []
    for y in range(2):
        for z in range(4):
            ty, tz = move(y, z)
            pairs.append((y * 4 + z, ty * 4 + tz))
    return lax.ppermute(value, "col", pairs)


def to_x(value, d):
    return row_perm(value, lambda y, x, e: (y, (x + d) % 4, e))


def to_ylo(value):
    return row_perm(value, lambda y, x, e: (1 - y, x, e))


def to_core(value):
    return row_perm(value, lambda y, x, e: (y, x, 1 - e))


def to_z(value, d):
    return col_perm(value, lambda y, z: (y, (z + d) % 4))


def to_yhi(value):
    return col_perm(value, lambda y, z: (1 - y, z))


def dense_kernel(places, tiles, panel_out, panel_t, held, panel, place_s, sems, place_sem, out_sem):
    place_copy = pltpu.make_async_copy(places, place_s, place_sem)
    place_copy.start()

    def fetch(q):
        part = pl.ds(q * CT, CT)
        return pltpu.make_async_copy(tiles.at[part], held.at[part], sems.at[q])

    for q in range(CHUNKS):
        fetch(q).start()

    def clear(j, _):
        panel[j] = jnp.zeros((ROWS * T, T), BF)
        return 0

    def clear_t(i, _):
        panel_t[i] = jnp.zeros((COLS * T, T), BF)
        return 0

    lax.fori_loop(0, COLS, clear, 0)
    place_copy.wait()
    count = place_s[0, CAP]

    def spot(s):
        at = place_s[0, s]
        return lax.div(at, COLS), lax.rem(at, COLS)

    def put(s):
        i, j = spot(s)
        panel[j, pl.ds(pl.multiple_of(i * T, T), T), :] = held[s]

    def put_t(s):
        i, j = spot(s)
        panel_t[i, pl.ds(pl.multiple_of(j * T, T), T), :] = held[s].T

    def each(low, live, step):
        def many(g, _):
            for u in range(UNROLL):
                step(low + g * UNROLL + u)
            return 0

        def one(s, _):
            step(s)
            return 0

        groups = lax.div(live, UNROLL)
        lax.fori_loop(0, groups, many, 0)
        lax.fori_loop(low + groups * UNROLL, low + live, one, 0)

    for q in range(CHUNKS):
        fetch(q).wait()
        each(q * CT, jnp.clip(count - q * CT, 0, CT), put)
    out_copy = pltpu.make_async_copy(panel, panel_out, out_sem)
    out_copy.start()
    lax.fori_loop(0, ROWS, clear_t, 0)
    each(0, count, put_t)
    out_copy.wait()


def slots(tile_row, tile_column, tile_count):
    spots = jnp.pad(tile_row * COLS + tile_column, ((0, 0), (0, T)))
    at = lax.broadcasted_iota(jnp.int32, spots.shape, 1)
    return jnp.where(at == CAP, tile_count[0], spots)


def dense(tiles, places):
    return pl.pallas_call(
        dense_kernel,
        out_shape=(
            SDS((COLS, ROWS * T, T), BF),
            pltpu.VMEM((ROWS, COLS * T, T), BF),
        ),
        in_specs=[HBM, HBM],
        out_specs=(HBM, VMEM),
        scratch_shapes=[
            pltpu.VMEM((CAP, T, T), BF),
            pltpu.VMEM((COLS, ROWS * T, T), BF),
            pltpu.SMEM((1, CAP + T), jnp.int32),
            pltpu.SemaphoreType.DMA((CHUNKS,)),
            pltpu.SemaphoreType.DMA,
            pltpu.SemaphoreType.DMA,
        ],
        compiler_params=pltpu.CompilerParams(vmem_limit_bytes=30 * MIB),
        cost_estimate=pl.CostEstimate(flops=0, bytes_accessed=45 * MIB, transcendentals=0),
        name="dense",
    )(places, tiles)


def row_place():
    r = lax.axis_index("row")
    return lax.div(r, 8), lax.rem(lax.div(r, 2), 4), lax.rem(r, 2)


def col_place():
    c = lax.axis_index("col")
    return lax.div(c, 4), lax.rem(c, 4)


def row_of(place, hop, flip, swap):
    y, x, e = place
    y = 1 - y if flip else y
    e = 1 - e if swap else e
    return (y * 4 + lax.rem(x + hop, 4)) * 2 + e


def col_of(place, hop, flip):
    y, z = place
    y = 1 - y if flip else y
    return y * 4 + lax.rem(z + hop, 4)


def block_rows(k):
    return pl.ds(pl.multiple_of(k * BLK, BLK), BLK)


def back_kernel(panel_t, *refs, targets):
    sources = refs[:4]
    outs = refs[4:]
    here, there = col_place(), row_place()
    rhs = jnp.concatenate([ref[...] for ref in sources], axis=0)
    order = []
    for hop in HOPS:
        for flip in range(2):
            c = col_of(here, (4 - hop) % 4, flip)
            order += [2 * c, 2 * c + 1]
    for n, (hop, swap) in enumerate(targets):
        lhs = []
        for flip in range(2):
            k = row_of(there, hop, flip, swap)
            part = block_rows(k)
            lhs.append(jnp.concatenate([panel_t[i, part, :] for i in order], axis=1))
        lhs = jnp.concatenate(lhs, axis=0)
        product = jnp.dot(lhs, rhs, preferred_element_type=F32)
        if len(outs) == 1:
            outs[0][n * 2 * BLK : (n + 1) * 2 * BLK, :] = product.astype(BF)
        else:
            outs[n][...] = product.astype(BF)


def back(panel_t, sources, targets, joined):
    n = len(targets)
    if joined:
        out_shape, out_specs = (SDS((n * 2 * BLK, BLK), BF),), (VMEM,)
    else:
        out_shape, out_specs = (SDS((2 * BLK, BLK), BF),) * n, (VMEM,) * n
    return pl.pallas_call(
        functools.partial(back_kernel, targets=targets),
        out_shape=out_shape,
        in_specs=[VMEM] * 5,
        out_specs=out_specs,
        compiler_params=pltpu.CompilerParams(vmem_limit_bytes=8 * MIB),
        cost_estimate=pl.CostEstimate(
            flops=2 * n * 512 * 2048 * 256, bytes_accessed=n * MIB, transcendentals=0
        ),
        name="back",
    )(panel_t, *sources)


def forward_kernel(panel, *refs, targets):
    sources = refs[:8]
    outs = refs[8:]
    here, there = col_place(), row_place()
    rhs = jnp.concatenate([ref[...] for ref in sources], axis=0)
    order = []
    for swap in range(2):
        for hop in HOPS:
            for flip in range(2):
                k = row_of(there, (4 - hop) % 4, flip, swap)
                order += [2 * k, 2 * k + 1]
    for (hop, flip), out in zip(targets, outs):
        part = block_rows(col_of(here, hop, flip))
        lhs = jnp.concatenate([panel[j, part, :] for j in order], axis=1)
        out[...] = jnp.dot(lhs, rhs, preferred_element_type=F32).astype(out.dtype)


def forward(panel, sources, targets, dtype=BF):
    n = len(targets)
    return pl.pallas_call(
        functools.partial(forward_kernel, targets=targets),
        out_shape=(SDS((BLK, BLK), dtype),) * n,
        in_specs=[VMEM] * 9,
        out_specs=(VMEM,) * n,
        compiler_params=pltpu.CompilerParams(vmem_limit_bytes=8 * MIB),
        cost_estimate=pl.CostEstimate(
            flops=2 * n * 256 * 4096 * 256, bytes_accessed=n * MIB // 2, transcendentals=0
        ),
        name="forward",
    )(panel, *sources)


def join_kernel(recv, *refs):
    own, outs = refs[:4], refs[4:]
    for n in range(4):
        part = recv[n * 2 * BLK : (n + 1) * 2 * BLK, :].astype(F32)
        outs[n][...] = (own[n][...].astype(F32) + part).astype(BF)


def join(recv, own):
    return pl.pallas_call(
        join_kernel,
        out_shape=(SDS((2 * BLK, BLK), BF),) * 4,
        in_specs=[VMEM] * 5,
        out_specs=(VMEM,) * 4,
        compiler_params=pltpu.CompilerParams(vmem_limit_bytes=4 * MIB),
        name="join",
    )(recv, *own)


def pair_kernel(x, high, low, row_pair, col_pair):
    row_pair[:BLK] = x[...]
    row_pair[BLK:] = high[...]
    col_pair[:BLK] = x[...]
    col_pair[BLK:] = low[...]


def pair(x, high, low):
    return pl.pallas_call(
        pair_kernel,
        out_shape=(SDS((2 * BLK, BLK), BF),) * 2,
        in_specs=[VMEM] * 3,
        out_specs=(VMEM,) * 2,
        compiler_params=pltpu.CompilerParams(vmem_limit_bytes=4 * MIB),
        name="pair",
    )(x, high, low)


def stage_kernel(x, out, sem):
    copy = pltpu.make_async_copy(x, out, sem)
    copy.start()
    copy.wait()


def stage(x):
    return pl.pallas_call(
        stage_kernel,
        out_shape=pltpu.VMEM(x.shape, x.dtype),
        in_specs=[HBM],
        out_specs=VMEM,
        scratch_shapes=[pltpu.SemaphoreType.DMA],
        compiler_params=pltpu.CompilerParams(vmem_limit_bytes=4 * MIB),
        name="stage",
    )(x)


def total_kernel(*refs):
    total = refs[0][...].astype(F32)
    for ref in refs[1:-1]:
        total = total + ref[...].astype(F32)
    refs[-1][...] = total.astype(BF)


def total(*parts):
    return pl.pallas_call(
        total_kernel,
        out_shape=SDS(parts[0].shape, BF),
        in_specs=[VMEM] * len(parts),
        out_specs=VMEM,
        compiler_params=pltpu.CompilerParams(vmem_limit_bytes=4 * MIB),
        name="total",
    )(*parts)


def fold_kernel(own, a, b, c, keep, send):
    total = own[...].astype(F32) + a[...].astype(F32) + b[...].astype(F32) + c[...].astype(F32)
    keep[...] = total[:BLK]
    send[...] = total[BLK:].astype(BF)


def fold(own, arrived):
    return pl.pallas_call(
        fold_kernel,
        out_shape=(SDS((BLK, BLK), F32), SDS((BLK, BLK), BF)),
        in_specs=[VMEM] * 4,
        out_specs=(VMEM, VMEM),
        compiler_params=pltpu.CompilerParams(vmem_limit_bytes=4 * MIB),
        name="fold",
    )(own, *arrived)


def update_kernel(*refs):
    x, parts = refs[0], refs[1:-5]
    w_in, b_in, w_out, b_out, out = refs[-5:]
    total = parts[0][...].astype(F32)
    for ref in parts[1:]:
        total = total + ref[...].astype(F32)
    combined = (x[...].astype(F32) + total).astype(BF)
    hidden = jnp.dot(combined, w_in[...], preferred_element_type=F32) + b_in[...]
    hidden = jnp.maximum(hidden, 0.0).astype(BF)
    updated = jnp.dot(hidden, w_out[...], preferred_element_type=F32) + b_out[...]
    out[...] = updated.astype(BF)


def update(x, parts, w_in, b_in, w_out, b_out):
    return pl.pallas_call(
        update_kernel,
        out_shape=SDS((BLK, BLK), BF),
        in_specs=[VMEM] * (len(parts) + 5),
        out_specs=VMEM,
        compiler_params=pltpu.CompilerParams(vmem_limit_bytes=6 * MIB),
        name="update",
    )(x, *parts, w_in, b_in.reshape(1, -1), w_out, b_out.reshape(1, -1))


def shards(
    features, adjacency, tile_row, tile_column, tile_count, weight_in, bias_in, weight_out, bias_out
):
    high, low = to_yhi(features), to_ylo(features)
    own_features = stage(features)
    places = slots(tile_row, tile_column, tile_count)
    own_features, places = lax.optimization_barrier((own_features, places))
    row_pair, col_pair = pair(own_features, high, low)
    row_pairs, col_pairs = [row_pair], [col_pair]
    for d in HOPS[1:]:
        col_pairs.append(to_x(col_pair, d))
        row_pairs.append(to_z(row_pair, d))

    places, _ = lax.optimization_barrier((places, (row_pair, col_pair)))
    panel, panel_t = dense(adjacency[0], places)
    col_pairs = col_pairs + [to_core(block) for block in col_pairs]

    (to_other,) = back(panel_t, row_pairs, tuple((h, 1) for h in HOPS), True)
    from_other = to_core(to_other)
    own = back(panel_t, row_pairs, tuple((h, 0) for h in HOPS), False)
    chip = join(from_other, own)
    arrived = [to_x(chip[n], HOPS[n]) for n in (1, 2, 3)]

    sent = [forward(panel, col_pairs, tuple((h, flip) for h in HOPS[1:])) for flip in (1, 0)]
    on, here = ([to_z(block, h) for block, h in zip(part, HOPS[1:])] for part in sent)
    stay, turn = forward(panel, col_pairs, ((0, 0), (0, 1)), F32)

    col_keep, col_send = fold(chip[0], arrived)
    col_recv = to_ylo(col_send)
    row_recv = to_yhi(total(turn, *on))
    return update(
        own_features,
        (stay, *here, row_recv, col_keep, col_recv),
        weight_in,
        bias_in,
        weight_out,
        bias_out,
    )


def solution(mesh):
    placed = (
        P(("row", "col"), None),
        P(("row", "col"), None, None, None),
        P(("row", "col"), None),
        P(("row", "col"), None),
        P(("row", "col")),
        P(),
        P(),
        P(),
        P(),
    )
    return jax.shard_map(
        shards, mesh=mesh, in_specs=placed, out_specs=P(("row", "col"), None), check_vma=False
    )
```

```python
import functools

import jax
import jax.numpy as jnp
from jax import lax
from jax.experimental import pallas as pl
from jax.experimental.pallas import tpu as pltpu
from jax.sharding import PartitionSpec as P


T = 128
BLK = 256
ROWS = 16
COLS = 32
CAP = 384
CHUNKS = 12
CT = CAP // CHUNKS
SLOTS = 6
UNROLL = 16
HOPS = (0, 1, 3, 2)
BF = jnp.bfloat16
F32 = jnp.float32
MIB = 2**20
VMEM = pl.BlockSpec(memory_space=pltpu.VMEM)
HBM = pl.BlockSpec(memory_space=pltpu.HBM)
SDS = jax.ShapeDtypeStruct


def row_perm(value, move):
    pairs = []
    for y in range(2):
        for x in range(4):
            for e in range(2):
                ty, tx, te = move(y, x, e)
                pairs.append(((y * 4 + x) * 2 + e, (ty * 4 + tx) * 2 + te))
    return lax.ppermute(value, "row", pairs)


def col_perm(value, move):
    pairs = []
    for y in range(2):
        for z in range(4):
            ty, tz = move(y, z)
            pairs.append((y * 4 + z, ty * 4 + tz))
    return lax.ppermute(value, "col", pairs)


def to_x(value, d):
    return row_perm(value, lambda y, x, e: (y, (x + d) % 4, e))


def to_ylo(value):
    return row_perm(value, lambda y, x, e: (1 - y, x, e))


def to_core(value):
    return row_perm(value, lambda y, x, e: (y, x, 1 - e))


def to_z(value, d):
    return col_perm(value, lambda y, z: (y, (z + d) % 4))


def to_yhi(value):
    return col_perm(value, lambda y, z: (1 - y, z))


def clear_kernel(panel, panel_t):
    def clear(j, _):
        panel[j] = jnp.zeros((ROWS * T, T), BF)
        return 0

    def clear_t(i, _):
        panel_t[i] = jnp.zeros((COLS * T, T), BF)
        return 0

    lax.fori_loop(0, COLS, clear, 0)
    lax.fori_loop(0, ROWS, clear_t, 0)


PANELS = (pltpu.VMEM((COLS, ROWS * T, T), BF), pltpu.VMEM((ROWS, COLS * T, T), BF))


def cleared():
    return pl.pallas_call(
        clear_kernel,
        out_shape=PANELS,
        out_specs=(VMEM, VMEM),
        compiler_params=pltpu.CompilerParams(vmem_limit_bytes=4 * MIB),
        cost_estimate=pl.CostEstimate(flops=0, bytes_accessed=12 * MIB, transcendentals=0),
        name="clear",
    )()


def dense_kernel(places, tiles, _, __, panel, panel_t, held, place_s, sems, place_sem):
    place_copy = pltpu.make_async_copy(places, place_s, place_sem)
    place_copy.start()

    def fetch(q):
        part = pl.ds(q * CT, CT)
        return pltpu.make_async_copy(tiles.at[part], held.at[q % SLOTS], sems.at[q % SLOTS])

    place_copy.wait()
    count = place_s[0, CAP]

    def begin(q):
        @pl.when(q * CT < count)
        def _():
            fetch(q).start()

    for q in range(SLOTS):
        begin(q)

    def place(s, slot, low):
        spot = place_s[0, s]
        i = lax.div(spot, COLS)
        j = lax.rem(spot, COLS)
        tile = held[slot, s - low]
        panel[j, pl.ds(pl.multiple_of(i * T, T), T), :] = tile
        panel_t[i, pl.ds(pl.multiple_of(j * T, T), T), :] = tile.T

    for q in range(CHUNKS):
        low = q * CT
        live = jnp.clip(count - low, 0, CT)

        @pl.when(low < count)
        def _(q=q):
            fetch(q).wait()

        def many(g, _, q=q, low=low):
            for u in range(UNROLL):
                place(low + g * UNROLL + u, q % SLOTS, low)
            return 0

        def one(s, _, q=q, low=low):
            place(s, q % SLOTS, low)
            return 0

        groups = lax.div(live, UNROLL)
        lax.fori_loop(0, groups, many, 0)
        lax.fori_loop(low + groups * UNROLL, low + live, one, 0)
        if q + SLOTS < CHUNKS:
            begin(q + SLOTS)


def slots(tile_row, tile_column, tile_count):
    spots = jnp.pad(tile_row * COLS + tile_column, ((0, 0), (0, T)))
    at = lax.broadcasted_iota(jnp.int32, spots.shape, 1)
    return jnp.where(at == CAP, tile_count[0], spots)


def dense(tiles, places, panels):
    return pl.pallas_call(
        dense_kernel,
        out_shape=PANELS,
        in_specs=[HBM, HBM, VMEM, VMEM],
        out_specs=(VMEM, VMEM),
        scratch_shapes=[
            pltpu.VMEM((SLOTS, CT, T, T), BF),
            pltpu.SMEM((1, CAP + T), jnp.int32),
            pltpu.SemaphoreType.DMA((SLOTS,)),
            pltpu.SemaphoreType.DMA,
        ],
        compiler_params=pltpu.CompilerParams(vmem_limit_bytes=12 * MIB),
        cost_estimate=pl.CostEstimate(flops=0, bytes_accessed=45 * MIB, transcendentals=0),
        input_output_aliases={2: 0, 3: 1},
        name="dense",
    )(places, tiles, *panels)


def row_place():
    r = lax.axis_index("row")
    return lax.div(r, 8), lax.rem(lax.div(r, 2), 4), lax.rem(r, 2)


def col_place():
    c = lax.axis_index("col")
    return lax.div(c, 4), lax.rem(c, 4)


def row_of(place, hop, flip, swap):
    y, x, e = place
    y = 1 - y if flip else y
    e = 1 - e if swap else e
    return (y * 4 + lax.rem(x + hop, 4)) * 2 + e


def col_of(place, hop, flip):
    y, z = place
    y = 1 - y if flip else y
    return y * 4 + lax.rem(z + hop, 4)


def block_rows(k):
    return pl.ds(pl.multiple_of(k * BLK, BLK), BLK)


def back_kernel(panel_t, *refs, targets):
    sources = refs[:4]
    outs = refs[4:]
    here, there = col_place(), row_place()
    rhs = jnp.concatenate([ref[...] for ref in sources], axis=0)
    order = []
    for hop in HOPS:
        for flip in range(2):
            c = col_of(here, (4 - hop) % 4, flip)
            order += [2 * c, 2 * c + 1]
    for n, (hop, swap) in enumerate(targets):
        lhs = []
        for flip in range(2):
            k = row_of(there, hop, flip, swap)
            part = block_rows(k)
            lhs.append(jnp.concatenate([panel_t[i, part, :] for i in order], axis=1))
        lhs = jnp.concatenate(lhs, axis=0)
        product = jnp.dot(lhs, rhs, preferred_element_type=F32)
        if len(outs) == 1:
            outs[0][n * 2 * BLK : (n + 1) * 2 * BLK, :] = product.astype(BF)
        else:
            outs[n][...] = product.astype(BF)


def back(panel_t, sources, targets, joined):
    n = len(targets)
    if joined:
        out_shape, out_specs = (SDS((n * 2 * BLK, BLK), BF),), (VMEM,)
    else:
        out_shape, out_specs = (SDS((2 * BLK, BLK), BF),) * n, (VMEM,) * n
    return pl.pallas_call(
        functools.partial(back_kernel, targets=targets),
        out_shape=out_shape,
        in_specs=[VMEM] * 5,
        out_specs=out_specs,
        compiler_params=pltpu.CompilerParams(vmem_limit_bytes=8 * MIB),
        cost_estimate=pl.CostEstimate(
            flops=2 * n * 512 * 2048 * 256, bytes_accessed=n * MIB, transcendentals=0
        ),
        name="back",
    )(panel_t, *sources)


def forward_kernel(panel, *refs, targets):
    sources = refs[:8]
    outs = refs[8:]
    here, there = col_place(), row_place()
    rhs = jnp.concatenate([ref[...] for ref in sources], axis=0)
    order = []
    for swap in range(2):
        for hop in HOPS:
            for flip in range(2):
                k = row_of(there, (4 - hop) % 4, flip, swap)
                order += [2 * k, 2 * k + 1]
    for (hop, flip), out in zip(targets, outs):
        part = block_rows(col_of(here, hop, flip))
        lhs = jnp.concatenate([panel[j, part, :] for j in order], axis=1)
        out[...] = jnp.dot(lhs, rhs, preferred_element_type=F32).astype(out.dtype)


def forward(panel, sources, targets, dtype=BF):
    n = len(targets)
    return pl.pallas_call(
        functools.partial(forward_kernel, targets=targets),
        out_shape=(SDS((BLK, BLK), dtype),) * n,
        in_specs=[VMEM] * 9,
        out_specs=(VMEM,) * n,
        compiler_params=pltpu.CompilerParams(vmem_limit_bytes=8 * MIB),
        cost_estimate=pl.CostEstimate(
            flops=2 * n * 256 * 4096 * 256, bytes_accessed=n * MIB // 2, transcendentals=0
        ),
        name="forward",
    )(panel, *sources)


def join_kernel(recv, *refs):
    own, outs = refs[:4], refs[4:]
    for n in range(4):
        part = recv[n * 2 * BLK : (n + 1) * 2 * BLK, :].astype(F32)
        outs[n][...] = (own[n][...].astype(F32) + part).astype(BF)


def join(recv, own):
    return pl.pallas_call(
        join_kernel,
        out_shape=(SDS((2 * BLK, BLK), BF),) * 4,
        in_specs=[VMEM] * 5,
        out_specs=(VMEM,) * 4,
        compiler_params=pltpu.CompilerParams(vmem_limit_bytes=4 * MIB),
        name="join",
    )(recv, *own)


def pair_kernel(x, high, low, row_pair, col_pair):
    row_pair[:BLK] = x[...]
    row_pair[BLK:] = high[...]
    col_pair[:BLK] = x[...]
    col_pair[BLK:] = low[...]


def pair(x, high, low):
    return pl.pallas_call(
        pair_kernel,
        out_shape=(SDS((2 * BLK, BLK), BF),) * 2,
        in_specs=[VMEM] * 3,
        out_specs=(VMEM,) * 2,
        compiler_params=pltpu.CompilerParams(vmem_limit_bytes=4 * MIB),
        name="pair",
    )(x, high, low)


def stage_kernel(x, out, sem):
    copy = pltpu.make_async_copy(x, out, sem)
    copy.start()
    copy.wait()


def stage(x):
    return pl.pallas_call(
        stage_kernel,
        out_shape=pltpu.VMEM(x.shape, x.dtype),
        in_specs=[HBM],
        out_specs=VMEM,
        scratch_shapes=[pltpu.SemaphoreType.DMA],
        compiler_params=pltpu.CompilerParams(vmem_limit_bytes=4 * MIB),
        name="stage",
    )(x)


def total_kernel(*refs):
    total = refs[0][...].astype(F32)
    for ref in refs[1:-1]:
        total = total + ref[...].astype(F32)
    refs[-1][...] = total.astype(BF)


def total(*parts):
    return pl.pallas_call(
        total_kernel,
        out_shape=SDS(parts[0].shape, BF),
        in_specs=[VMEM] * len(parts),
        out_specs=VMEM,
        compiler_params=pltpu.CompilerParams(vmem_limit_bytes=4 * MIB),
        name="total",
    )(*parts)


def fold_kernel(own, a, b, c, keep, send):
    total = own[...].astype(F32) + a[...].astype(F32) + b[...].astype(F32) + c[...].astype(F32)
    keep[...] = total[:BLK]
    send[...] = total[BLK:].astype(BF)


def fold(own, arrived):
    return pl.pallas_call(
        fold_kernel,
        out_shape=(SDS((BLK, BLK), F32), SDS((BLK, BLK), BF)),
        in_specs=[VMEM] * 4,
        out_specs=(VMEM, VMEM),
        compiler_params=pltpu.CompilerParams(vmem_limit_bytes=4 * MIB),
        name="fold",
    )(own, *arrived)


def update_kernel(*refs):
    x, parts = refs[0], refs[1:-5]
    w_in, b_in, w_out, b_out, out = refs[-5:]
    total = parts[0][...].astype(F32)
    for ref in parts[1:]:
        total = total + ref[...].astype(F32)
    combined = (x[...].astype(F32) + total).astype(BF)
    hidden = jnp.dot(combined, w_in[...], preferred_element_type=F32) + b_in[...]
    hidden = jnp.maximum(hidden, 0.0).astype(BF)
    updated = jnp.dot(hidden, w_out[...], preferred_element_type=F32) + b_out[...]
    out[...] = updated.astype(BF)


def update(x, parts, w_in, b_in, w_out, b_out):
    return pl.pallas_call(
        update_kernel,
        out_shape=SDS((BLK, BLK), BF),
        in_specs=[VMEM] * (len(parts) + 5),
        out_specs=VMEM,
        compiler_params=pltpu.CompilerParams(vmem_limit_bytes=6 * MIB),
        name="update",
    )(x, *parts, w_in, b_in.reshape(1, -1), w_out, b_out.reshape(1, -1))


def shards(
    features, adjacency, tile_row, tile_column, tile_count, weight_in, bias_in, weight_out, bias_out
):
    high = to_yhi(features)
    low = to_ylo(features)
    panels = cleared()
    own_features = stage(features)
    places = slots(tile_row, tile_column, tile_count)
    own_features, places = lax.optimization_barrier((own_features, places))
    row_pair, col_pair = pair(own_features, high, low)
    row_pairs, col_pairs = [row_pair], [col_pair]
    for d in HOPS[1:]:
        col_pairs.append(to_x(col_pair, d))
        row_pairs.append(to_z(row_pair, d))

    places, _ = lax.optimization_barrier((places, (row_pair, col_pair)))
    panel, panel_t = dense(adjacency[0], places, panels)
    col_pairs = col_pairs + [to_core(block) for block in col_pairs]

    (to_other,) = back(panel_t, row_pairs, tuple((h, 1) for h in HOPS), True)
    from_other = to_core(to_other)
    own = back(panel_t, row_pairs, tuple((h, 0) for h in HOPS), False)
    chip = join(from_other, own)
    arrived = [to_x(chip[n], HOPS[n]) for n in (1, 2, 3)]

    sent = [forward(panel, col_pairs, tuple((h, flip) for h in HOPS[1:])) for flip in (1, 0)]
    on, here = ([to_z(block, h) for block, h in zip(part, HOPS[1:])] for part in sent)
    stay, turn = forward(panel, col_pairs, ((0, 0), (0, 1)), F32)

    col_keep, col_send = fold(chip[0], arrived)
    col_recv = to_ylo(col_send)
    row_recv = to_yhi(total(turn, *on))
    return update(
        own_features,
        (stay, *here, row_recv, col_keep, col_recv),
        weight_in,
        bias_in,
        weight_out,
        bias_out,
    )


def solution(mesh):
    placed = (
        P(("row", "col"), None),
        P(("row", "col"), None, None, None),
        P(("row", "col"), None),
        P(("row", "col"), None),
        P(("row", "col")),
        P(),
        P(),
        P(),
        P(),
    )
    return jax.shard_map(
        shards, mesh=mesh, in_specs=placed, out_specs=P(("row", "col"), None), check_vma=False
    )
```

```python
import functools

import jax
import jax.numpy as jnp
from jax import lax
from jax.experimental import pallas as pl
from jax.experimental.pallas import tpu as pltpu
from jax.sharding import PartitionSpec as P


T = 128
BLK = 256
ROWS = 16
COLS = 32
CAP = 384
CHUNKS = 12
CT = CAP // CHUNKS
SLOTS = 6
UNROLL = 16
HOPS = (0, 1, 3, 2)
BF = jnp.bfloat16
F32 = jnp.float32
MIB = 2**20
VMEM = pl.BlockSpec(memory_space=pltpu.VMEM)
HBM = pl.BlockSpec(memory_space=pltpu.HBM)
SDS = jax.ShapeDtypeStruct


def row_perm(value, move):
    pairs = []
    for y in range(2):
        for x in range(4):
            for e in range(2):
                ty, tx, te = move(y, x, e)
                pairs.append(((y * 4 + x) * 2 + e, (ty * 4 + tx) * 2 + te))
    return lax.ppermute(value, "row", pairs)


def col_perm(value, move):
    pairs = []
    for y in range(2):
        for z in range(4):
            ty, tz = move(y, z)
            pairs.append((y * 4 + z, ty * 4 + tz))
    return lax.ppermute(value, "col", pairs)


def to_x(value, d):
    return row_perm(value, lambda y, x, e: (y, (x + d) % 4, e))


def to_ylo(value):
    return row_perm(value, lambda y, x, e: (1 - y, x, e))


def to_core(value):
    return row_perm(value, lambda y, x, e: (y, x, 1 - e))


def to_z(value, d):
    return col_perm(value, lambda y, z: (y, (z + d) % 4))


def to_yhi(value):
    return col_perm(value, lambda y, z: (1 - y, z))


def clear_kernel(_, panel, panel_t):
    def clear(j, _):
        panel[j] = jnp.zeros((ROWS * T, T), BF)
        return 0

    def clear_t(i, _):
        panel_t[i] = jnp.zeros((COLS * T, T), BF)
        return 0

    lax.fori_loop(0, COLS, clear, 0)
    lax.fori_loop(0, ROWS, clear_t, 0)


PANELS = (pltpu.VMEM((COLS, ROWS * T, T), BF), pltpu.VMEM((ROWS, COLS * T, T), BF))


def cleared(after):
    return pl.pallas_call(
        clear_kernel,
        out_shape=PANELS,
        in_specs=[VMEM],
        out_specs=(VMEM, VMEM),
        compiler_params=pltpu.CompilerParams(vmem_limit_bytes=4 * MIB),
        cost_estimate=pl.CostEstimate(flops=0, bytes_accessed=12 * MIB, transcendentals=0),
        name="clear",
    )(after)


def dense_kernel(places, tiles, _, __, panel, panel_t, held, place_s, sems, place_sem):
    place_copy = pltpu.make_async_copy(places, place_s, place_sem)
    place_copy.start()

    def fetch(q):
        part = pl.ds(q * CT, CT)
        return pltpu.make_async_copy(tiles.at[part], held.at[q % SLOTS], sems.at[q % SLOTS])

    place_copy.wait()
    count = place_s[0, CAP]

    def begin(q):
        @pl.when(q * CT < count)
        def _():
            fetch(q).start()

    for q in range(SLOTS):
        begin(q)

    def place(s, slot, low):
        spot = place_s[0, s]
        i = lax.div(spot, COLS)
        j = lax.rem(spot, COLS)
        tile = held[slot, s - low]
        panel[j, pl.ds(pl.multiple_of(i * T, T), T), :] = tile
        panel_t[i, pl.ds(pl.multiple_of(j * T, T), T), :] = tile.T

    for q in range(CHUNKS):
        low = q * CT
        live = jnp.clip(count - low, 0, CT)

        @pl.when(low < count)
        def _(q=q):
            fetch(q).wait()

        def many(g, _, q=q, low=low):
            for u in range(UNROLL):
                place(low + g * UNROLL + u, q % SLOTS, low)
            return 0

        def one(s, _, q=q, low=low):
            place(s, q % SLOTS, low)
            return 0

        groups = lax.div(live, UNROLL)
        lax.fori_loop(0, groups, many, 0)
        lax.fori_loop(low + groups * UNROLL, low + live, one, 0)
        if q + SLOTS < CHUNKS:
            begin(q + SLOTS)


def slots(tile_row, tile_column, tile_count):
    spots = jnp.pad(tile_row * COLS + tile_column, ((0, 0), (0, T)))
    at = lax.broadcasted_iota(jnp.int32, spots.shape, 1)
    return jnp.where(at == CAP, tile_count[0], spots)


def dense(tiles, places, panels):
    return pl.pallas_call(
        dense_kernel,
        out_shape=PANELS,
        in_specs=[HBM, HBM, VMEM, VMEM],
        out_specs=(VMEM, VMEM),
        scratch_shapes=[
            pltpu.VMEM((SLOTS, CT, T, T), BF),
            pltpu.SMEM((1, CAP + T), jnp.int32),
            pltpu.SemaphoreType.DMA((SLOTS,)),
            pltpu.SemaphoreType.DMA,
        ],
        compiler_params=pltpu.CompilerParams(vmem_limit_bytes=12 * MIB),
        cost_estimate=pl.CostEstimate(flops=0, bytes_accessed=45 * MIB, transcendentals=0),
        input_output_aliases={2: 0, 3: 1},
        name="dense",
    )(places, tiles, *panels)


def row_place():
    r = lax.axis_index("row")
    return lax.div(r, 8), lax.rem(lax.div(r, 2), 4), lax.rem(r, 2)


def col_place():
    c = lax.axis_index("col")
    return lax.div(c, 4), lax.rem(c, 4)


def row_of(place, hop, flip, swap):
    y, x, e = place
    y = 1 - y if flip else y
    e = 1 - e if swap else e
    return (y * 4 + lax.rem(x + hop, 4)) * 2 + e


def col_of(place, hop, flip):
    y, z = place
    y = 1 - y if flip else y
    return y * 4 + lax.rem(z + hop, 4)


def block_rows(k):
    return pl.ds(pl.multiple_of(k * BLK, BLK), BLK)


def back_kernel(panel_t, *refs, targets):
    sources = refs[:4]
    outs = refs[4:]
    here, there = col_place(), row_place()
    rhs = jnp.concatenate([ref[...] for ref in sources], axis=0)
    order = []
    for hop in HOPS:
        for flip in range(2):
            c = col_of(here, (4 - hop) % 4, flip)
            order += [2 * c, 2 * c + 1]
    for n, (hop, swap) in enumerate(targets):
        lhs = []
        for flip in range(2):
            k = row_of(there, hop, flip, swap)
            part = block_rows(k)
            lhs.append(jnp.concatenate([panel_t[i, part, :] for i in order], axis=1))
        lhs = jnp.concatenate(lhs, axis=0)
        product = jnp.dot(lhs, rhs, preferred_element_type=F32)
        if len(outs) == 1:
            outs[0][n * 2 * BLK : (n + 1) * 2 * BLK, :] = product.astype(BF)
        else:
            outs[n][...] = product.astype(BF)


def back(panel_t, sources, targets, joined):
    n = len(targets)
    if joined:
        out_shape, out_specs = (SDS((n * 2 * BLK, BLK), BF),), (VMEM,)
    else:
        out_shape, out_specs = (SDS((2 * BLK, BLK), BF),) * n, (VMEM,) * n
    return pl.pallas_call(
        functools.partial(back_kernel, targets=targets),
        out_shape=out_shape,
        in_specs=[VMEM] * 5,
        out_specs=out_specs,
        compiler_params=pltpu.CompilerParams(vmem_limit_bytes=8 * MIB),
        cost_estimate=pl.CostEstimate(
            flops=2 * n * 512 * 2048 * 256, bytes_accessed=n * MIB, transcendentals=0
        ),
        name="back",
    )(panel_t, *sources)


def forward_kernel(panel, *refs, targets):
    sources = refs[:8]
    outs = refs[8:]
    here, there = col_place(), row_place()
    rhs = jnp.concatenate([ref[...] for ref in sources], axis=0)
    order = []
    for swap in range(2):
        for hop in HOPS:
            for flip in range(2):
                k = row_of(there, (4 - hop) % 4, flip, swap)
                order += [2 * k, 2 * k + 1]
    for (hop, flip), out in zip(targets, outs):
        part = block_rows(col_of(here, hop, flip))
        lhs = jnp.concatenate([panel[j, part, :] for j in order], axis=1)
        out[...] = jnp.dot(lhs, rhs, preferred_element_type=F32).astype(out.dtype)


def forward(panel, sources, targets, dtype=BF):
    n = len(targets)
    return pl.pallas_call(
        functools.partial(forward_kernel, targets=targets),
        out_shape=(SDS((BLK, BLK), dtype),) * n,
        in_specs=[VMEM] * 9,
        out_specs=(VMEM,) * n,
        compiler_params=pltpu.CompilerParams(vmem_limit_bytes=8 * MIB),
        cost_estimate=pl.CostEstimate(
            flops=2 * n * 256 * 4096 * 256, bytes_accessed=n * MIB // 2, transcendentals=0
        ),
        name="forward",
    )(panel, *sources)


def join_kernel(recv, *refs):
    own, outs = refs[:4], refs[4:]
    for n in range(4):
        part = recv[n * 2 * BLK : (n + 1) * 2 * BLK, :].astype(F32)
        outs[n][...] = (own[n][...].astype(F32) + part).astype(BF)


def join(recv, own):
    return pl.pallas_call(
        join_kernel,
        out_shape=(SDS((2 * BLK, BLK), BF),) * 4,
        in_specs=[VMEM] * 5,
        out_specs=(VMEM,) * 4,
        compiler_params=pltpu.CompilerParams(vmem_limit_bytes=4 * MIB),
        name="join",
    )(recv, *own)


def pair_kernel(x, high, low, row_pair, col_pair):
    row_pair[:BLK] = x[...]
    row_pair[BLK:] = high[...]
    col_pair[:BLK] = x[...]
    col_pair[BLK:] = low[...]


def pair(x, high, low):
    return pl.pallas_call(
        pair_kernel,
        out_shape=(SDS((2 * BLK, BLK), BF),) * 2,
        in_specs=[VMEM] * 3,
        out_specs=(VMEM,) * 2,
        compiler_params=pltpu.CompilerParams(vmem_limit_bytes=4 * MIB),
        name="pair",
    )(x, high, low)


def total_kernel(*refs):
    total = refs[0][...].astype(F32)
    for ref in refs[1:-1]:
        total = total + ref[...].astype(F32)
    refs[-1][...] = total.astype(BF)


def total(*parts):
    return pl.pallas_call(
        total_kernel,
        out_shape=SDS(parts[0].shape, BF),
        in_specs=[VMEM] * len(parts),
        out_specs=VMEM,
        compiler_params=pltpu.CompilerParams(vmem_limit_bytes=4 * MIB),
        name="total",
    )(*parts)


def fold_kernel(own, a, b, c, keep, send):
    total = own[...].astype(F32) + a[...].astype(F32) + b[...].astype(F32) + c[...].astype(F32)
    keep[...] = total[:BLK]
    send[...] = total[BLK:].astype(BF)


def fold(own, arrived):
    return pl.pallas_call(
        fold_kernel,
        out_shape=(SDS((BLK, BLK), F32), SDS((BLK, BLK), BF)),
        in_specs=[VMEM] * 4,
        out_specs=(VMEM, VMEM),
        compiler_params=pltpu.CompilerParams(vmem_limit_bytes=4 * MIB),
        name="fold",
    )(own, *arrived)


def update_kernel(*refs):
    x, parts = refs[0], refs[1:-5]
    w_in, b_in, w_out, b_out, out = refs[-5:]
    total = parts[0][...].astype(F32)
    for ref in parts[1:]:
        total = total + ref[...].astype(F32)
    combined = (x[...].astype(F32) + total).astype(BF)
    hidden = jnp.dot(combined, w_in[...], preferred_element_type=F32) + b_in[...]
    hidden = jnp.maximum(hidden, 0.0).astype(BF)
    updated = jnp.dot(hidden, w_out[...], preferred_element_type=F32) + b_out[...]
    out[...] = updated.astype(BF)


def update(x, parts, w_in, b_in, w_out, b_out):
    return pl.pallas_call(
        update_kernel,
        out_shape=SDS((BLK, BLK), BF),
        in_specs=[VMEM] * (len(parts) + 5),
        out_specs=VMEM,
        compiler_params=pltpu.CompilerParams(vmem_limit_bytes=6 * MIB),
        name="update",
    )(x, *parts, w_in, b_in.reshape(1, -1), w_out, b_out.reshape(1, -1))


def shards(
    features, adjacency, tile_row, tile_column, tile_count, weight_in, bias_in, weight_out, bias_out
):
    mine = lax.reduce_precision(features, 8, 7)
    high = to_yhi(features)
    low = to_ylo(features)
    panels = cleared(mine)
    row_pair, col_pair = pair(mine, high, low)
    row_pairs, col_pairs = [row_pair], [col_pair]
    for d in HOPS[1:]:
        col_pairs.append(to_x(col_pair, d))
        row_pairs.append(to_z(row_pair, d))

    indices, _ = lax.optimization_barrier(((tile_row, tile_column, tile_count), (row_pair, col_pair)))
    places = slots(*indices)
    panel, panel_t = dense(adjacency[0], places, panels)
    col_pairs = col_pairs + [to_core(block) for block in col_pairs]

    (to_other,) = back(panel_t, row_pairs, tuple((h, 1) for h in HOPS), True)
    from_other = to_core(to_other)
    own = back(panel_t, row_pairs, tuple((h, 0) for h in HOPS), False)
    chip = join(from_other, own)
    arrived = []
    for n in (1, 2, 3):
        arrived.append(to_x(chip[n], HOPS[n]))

    sent = [forward(panel, col_pairs, tuple((h, flip) for h in HOPS[1:])) for flip in (1, 0)]
    on, here = [], []
    for h, block in zip(HOPS[1:], sent[0]):
        on.append(to_z(block, h))
    for h, block in zip(HOPS[1:], sent[1]):
        here.append(to_z(block, h))
    (turn,) = forward(panel, col_pairs, ((0, 1),), F32)
    (stay,) = forward(panel, col_pairs, ((0, 0),), F32)

    col_keep, col_send = fold(chip[0], arrived)
    col_recv = to_ylo(col_send)
    onward = total(turn, *on)
    row_recv = to_yhi(onward)
    return update(
        mine,
        (stay, *here, row_recv, col_keep, col_recv),
        weight_in,
        bias_in,
        weight_out,
        bias_out,
    )


def solution(mesh):
    placed = (
        P(("row", "col"), None),
        P(("row", "col"), None, None, None),
        P(("row", "col"), None),
        P(("row", "col"), None),
        P(("row", "col")),
        P(),
        P(),
        P(),
        P(),
    )
    return jax.shard_map(
        shards, mesh=mesh, in_specs=placed, out_specs=P(("row", "col"), None), check_vma=False
    )
```
